32 devices in a mesh: grp: 2 (over x), bus: 16 (over z, y, core).
Axes of the slice: x: 2, y: 2, z: 4, core: 2. Of those that a mesh axis runs over, the one named last changes fastest.
Arguments:
- series: bfloat16 [32, 2048, 1024], P(('grp', 'bus')), parts along dimension 0, may hold values from -6 to 6
- hour_ids: int32 [32], P(('grp', 'bus')), parts along dimension 0, may hold values from 0 to 23
- hour_table: bfloat16 [24, 1024], replicated, may hold values from -3 to 3
- norm_gain: float32 [1024], replicated, may hold values from 0.1 to 1.9
- bus_order: int32 [4096], P('grp'), parts along dimension 0, may hold values from 0 to 2047, each once
- w_query: bfloat16 [1024, 512], replicated, may hold values from -0.1875 to 0.1875
- w_key: bfloat16 [1024, 512], replicated, may hold values from -0.1875 to 0.1875
- w_value: bfloat16 [1024, 512], replicated, may hold values from -0.1875 to 0.1875
- score_scale: float32 [8], replicated, may hold values from 0.5 to 10, as said below
- neighbors: int32 [32, 3], P('grp'), parts along dimension 0, may hold values from -1 to 15, as said below
- grad_out: bfloat16 [32, 2048, 512], P('grp', 'bus'), parts along dimension 0, may hold values from -6 to 6
Outputs:
- key_grad: bfloat16 [32, 2048, 512], P('grp', 'bus'), parts along dimension 0
- value_grad: bfloat16 [32, 2048, 512], P('grp', 'bus'), parts along dimension 0
The draws below stay inside these ranges and needn't reach their ends.
There are 2 independent parts, one for each index of `grp`. The reference program is written for one: setup_inputs(seed, part) draws one part's arguments, and reference() takes and returns one part's arrays. A program takes and returns all parts, laid end to end along the dimension named above; an argument that names none is the same for every part. Nothing has to cross between parts.
Inputs may be any that keep to these rules, and one draw needn't show every extreme that they name: `neighbors`: row b lists the key blocks read by query block b: entry 0 is b - 1 or -1, entry 1 is b, entry 2 is b + 1 or -1; -1 marks a block not read, and stands in entry 0 of row 0 and entry 2 of row 15. `score_scale`: positive temperatures of the heads.
All inputs are finite; a program needn't handle non-finite values.
Results may differ from the reference program's by a relative error of at most 0.018.
The reference program's roundings to bfloat16 on the way (of `normed`, `weights_b`, `attended` and `dscores`) count: a program that leaves them out, or rounds other values in their place, can miss the bound.
Values may be sent and summed in bfloat16 or wider, within the bound.
No kernel may reach another device: no remote copies, remote signals or barrier semaphores. Data moves between devices by JAX's collectives and lax.ppermute only.
A program may use at most 256 MiB of HBM per device.

```python
import math
import jax
import jax.numpy as jnp
from jax import lax

D = 1024
HEADS = 8
DH = 64
HOURS = 24
BLK = 128
SNAP = 16
NBLK = 16
BUS = 2048


def draw_score_scale(key, part):
    logs = jax.random.uniform(key, (HEADS,), jnp.float32, math.log(0.5), math.log(2.0))
    return jnp.exp(logs).astype(jnp.float32)


def draw_neighbors(key, part):
    block_ids = jnp.arange(NBLK, dtype=jnp.int32)
    keep = jax.random.randint(jax.random.fold_in(key, 7), (NBLK, 2), 0, 4) > 0
    lower = jnp.where(keep[:, 0] & (block_ids > 0), block_ids - 1, -1)
    upper = jnp.where(keep[:, 1] & (block_ids < NBLK - 1), block_ids + 1, -1)
    return jnp.stack([lower, block_ids, upper], axis=1).astype(jnp.int32)


def touch_ends(drawn, key, low, largest):
    extent = drawn.shape
    index_at = [jax.random.randint(jax.random.fold_in(key, axis), (), 0, extent[axis]) for axis in range(len(extent))]
    drawn = drawn.at[tuple(index_at)].set(low)
    longest = extent.index(max(extent))
    index_at[longest] = (index_at[longest] + 1) % extent[longest]
    return drawn.at[tuple(index_at)].set(largest)


def block_levels(own_key, extent, pieces, smallest, top_value):
    level, own = 1.0, jax.random.fold_in(own_key, 6)
    for axis_at, parts in pieces:
        draws = jnp.exp(jax.random.uniform(jax.random.fold_in(own, axis_at), (parts,), jnp.float32, smallest / len(pieces), top_value / len(pieces)))
        level = level * jnp.repeat(draws, extent[axis_at] // parts).reshape([-1 if axis == axis_at else 1 for axis in range(len(extent))])
    return level


def bell_draw(own_key, extent, width, most, shards=(), kind=jnp.bfloat16):
    gain = block_levels(own_key, extent, shards, -0.22, 0.18) if shards else 1.0
    values = jax.random.normal(own_key, extent, jnp.float32) * width * gain
    return jnp.minimum(jnp.maximum(values, -most), most).astype(kind)


def setup_inputs(seed: int = 0, part: int = 0) -> dict:
    streams_of = jax.random.split(jax.random.key(seed), 12)
    part_splits = jax.random.split(jax.random.fold_in(streams_of[11], part), 12)
    return {
        "series": bell_draw(part_splits[0], (SNAP, BUS, D), 1.0, 6.0, ((0, 16),)),
        "hour_ids": touch_ends(jax.random.randint(part_splits[1], (SNAP,), 0, HOURS), jax.random.fold_in(part_splits[1], 1), 0, HOURS - 1).astype(jnp.int32),
        "hour_table": bell_draw(streams_of[2], (HOURS, D), 0.5, 3.0),
        "norm_gain": jnp.clip(1.0 + 0.18 * jax.random.normal(streams_of[3], (D,), jnp.float32), 0.1, 1.9),
        "bus_order": jax.random.permutation(part_splits[4], BUS).astype(jnp.int32),
        "w_query": bell_draw(streams_of[5], (D, HEADS * DH), D ** -0.5, 0.1875),
        "w_key": bell_draw(streams_of[6], (D, HEADS * DH), D ** -0.5, 0.1875),
        "w_value": bell_draw(streams_of[7], (D, HEADS * DH), D ** -0.5, 0.1875),
        "score_scale": draw_score_scale(jax.random.fold_in(streams_of[11], 71), part),
        "neighbors": draw_neighbors(jax.random.fold_in(jax.random.fold_in(streams_of[11], part), 71), part),
        "grad_out": bell_draw(part_splits[10], (SNAP, BUS, HEADS * DH), 1.0, 6.0, ((1, 16),)),
    }


EPSILON = 1e-05
NEG_FILL = -1e+30

def reference(series, hour_ids, hour_table, norm_gain, bus_order, w_query, w_key, w_value, score_scale, neighbors, grad_out):
    feat_width = HEADS * DH
    ordered = jnp.take(series, bus_order, axis=1).astype(jnp.float32)
    hour_rows = jnp.take(hour_table, hour_ids, axis=0).astype(jnp.float32)
    mixed = ordered + hour_rows[:, None, :]
    normed = (mixed * lax.rsqrt(lax.optimization_barrier(jnp.mean(mixed * mixed, axis=-1, keepdims=True)) + EPSILON) * norm_gain).astype(jnp.bfloat16)
    flat_rows = normed.reshape(SNAP * BUS, D)

    def project(weight):
        product = jnp.dot(flat_rows, weight, preferred_element_type=jnp.float32).astype(jnp.bfloat16)
        return product.reshape(SNAP, NBLK, BLK, HEADS, DH)
    queries = project(w_query)
    key_rows = project(w_key)
    value_rows = project(w_value)
    grad_rows = grad_out.reshape(SNAP, NBLK, BLK, HEADS, DH)
    head_scale = (score_scale / math.sqrt(DH)).astype(jnp.float32)

    def block_terms(block):
        block_ids = neighbors[block]
        valid = block_ids >= 0
        safe_ids = jnp.where(valid, block_ids, 0).astype(jnp.int32)
        query_block = queries[:, block].astype(jnp.float32)
        grad_block = grad_rows[:, block].astype(jnp.float32)
        key_tiles = key_rows[:, safe_ids].reshape(SNAP, 3 * BLK, HEADS, DH).astype(jnp.float32)
        value_tiles = value_rows[:, safe_ids].reshape(SNAP, 3 * BLK, HEADS, DH).astype(jnp.float32)
        colvalid = jnp.repeat(valid, BLK)
        scores = jnp.einsum('sihd,sjhd->shij', query_block, key_tiles) * head_scale[None, :, None, None]
        scores = jnp.where(colvalid[None, None, None, :], scores, NEG_FILL)
        row_max = lax.optimization_barrier(jnp.max(scores, axis=-1))
        log_total = row_max + jnp.log(lax.optimization_barrier(jnp.sum(jnp.exp(scores - row_max[..., None]), axis=-1)))
        weights = jnp.exp(scores - log_total[..., None])
        weights_b = lax.optimization_barrier(weights.astype(jnp.bfloat16)).astype(jnp.float32)
        attended = jnp.einsum('shij,sjhd->sihd', weights_b, value_tiles)
        attended = lax.optimization_barrier(attended.astype(jnp.bfloat16)).astype(jnp.float32)
        row_dot = jnp.einsum('sihd,sihd->shi', grad_block, attended)
        dweights = jnp.einsum('sihd,sjhd->shij', grad_block, value_tiles)
        dscores = weights * (dweights - row_dot[..., None]) * head_scale[None, :, None, None]
        dscores = lax.optimization_barrier(dscores.astype(jnp.bfloat16)).astype(jnp.float32)
        value_part = jnp.einsum('shij,sihd->sjhd', weights_b, grad_block).astype(jnp.bfloat16)
        key_part = jnp.einsum('shij,sihd->sjhd', dscores, query_block).astype(jnp.bfloat16)
        key_part = key_part.reshape(SNAP, 3, BLK, feat_width).transpose(1, 0, 2, 3)
        value_part = value_part.reshape(SNAP, 3, BLK, feat_width).transpose(1, 0, 2, 3)
        return (key_part, value_part)

    def accumulate(carry, block):
        key_acc, value_acc = carry
        key_part, value_part = block_terms(block)
        key_part = lax.optimization_barrier(key_part)
        value_part = lax.optimization_barrier(value_part)
        block_ids = neighbors[block]
        target = jnp.where(block_ids >= 0, block_ids, NBLK).astype(jnp.int32)
        key_acc = key_acc.at[target].add(key_part.astype(jnp.float32))
        value_acc = value_acc.at[target].add(value_part.astype(jnp.float32))
        return ((key_acc, value_acc), None)
    empty = jnp.zeros((NBLK + 1, SNAP, BLK, feat_width), jnp.float32)
    (key_acc, value_acc), _ = lax.scan(accumulate, (empty, empty), jnp.arange(NBLK, dtype=jnp.int32))
    key_grad = key_acc[:NBLK].transpose(1, 0, 2, 3).reshape(SNAP, BUS, feat_width).astype(jnp.bfloat16)
    value_grad = value_acc[:NBLK].transpose(1, 0, 2, 3).reshape(SNAP, BUS, feat_width).astype(jnp.bfloat16)
    return (key_grad, value_grad)
```

```python
import functools
import math

import jax
import jax.numpy as jnp
from jax import lax
from jax.experimental import pallas as pl
from jax.experimental.pallas import tpu as pltpu
from jax.sharding import PartitionSpec as P

EPSILON = 1e-05
NEG_FILL = -1e30


def nt_dot(a, b):
    return lax.dot_general(a, b, (((1,), (1,)), ((), ())), preferred_element_type=jnp.float32)


def tn_dot(a, b):
    return lax.dot_general(a, b, (((0,), (0,)), ((), ())), preferred_element_type=jnp.float32)


def encode_kernel(
    hour_ref, order_ref, series_ref, table_ref, gain_ref, wq_ref, wk_ref, wv_ref, q_ref, k_ref, v_ref
):
    tile = order_ref.shape[0]
    buses = series_ref.shape[0]
    hours = table_ref.shape[0]
    pick = lax.broadcasted_iota(jnp.int32, (tile, buses), 1) == order_ref[...]
    ordered = jnp.dot(
        pick.astype(jnp.bfloat16), series_ref[...], preferred_element_type=jnp.float32
    )
    table = table_ref[...].astype(jnp.float32)
    is_hour = lax.broadcasted_iota(jnp.int32, (hours, 1), 0) == hour_ref[0]
    hour_row = jnp.sum(jnp.where(is_hour, table, 0.0), axis=0, keepdims=True)
    mixed = ordered + hour_row
    power = jnp.mean(mixed * mixed, axis=1, keepdims=True)
    normed = (mixed * lax.rsqrt(power + EPSILON) * gain_ref[...]).astype(jnp.bfloat16)
    for weight_ref, out_ref in ((wq_ref, q_ref), (wk_ref, k_ref), (wv_ref, v_ref)):
        out_ref[...] = jnp.dot(
            normed, weight_ref[...], preferred_element_type=jnp.float32
        ).astype(jnp.bfloat16)


def encode(series, hour_ids, hour_table, norm_gain, order, w_query, w_key, w_value, tile):
    buses, width = series.shape
    feat = w_query.shape[1]
    whole = lambda shape: pl.BlockSpec(shape, lambda i, *_: (0, 0))
    row_spec = pl.BlockSpec((tile, feat), lambda i, *_: (i, 0))
    out = jax.ShapeDtypeStruct((buses, feat), jnp.bfloat16)
    return pl.pallas_call(
        encode_kernel,
        grid_spec=pltpu.PrefetchScalarGridSpec(
            num_scalar_prefetch=1,
            grid=(buses // tile,),
            in_specs=[
                pl.BlockSpec((tile, 1), lambda i, *_: (i, 0)),
                whole((buses, width)),
                whole(hour_table.shape),
                whole((1, width)),
                whole((width, feat)),
                whole((width, feat)),
                whole((width, feat)),
            ],
            out_specs=[row_spec, row_spec, row_spec],
        ),
        out_shape=[out, out, out],
        compiler_params=pltpu.CompilerParams(vmem_limit_bytes=48 << 20),
        cost_estimate=pl.CostEstimate(
            flops=2 * buses * width * (buses + 3 * feat),
            bytes_accessed=2 * (buses * width + 3 * width * feat + 3 * buses * feat),
            transcendentals=buses,
        ),
        name="encode",
    )(
        hour_ids,
        order.reshape(buses, 1),
        series,
        hour_table,
        norm_gain.reshape(1, width),
        w_query,
        w_key,
        w_value,
    )


def attend_kernel(
    rows, neighbors_ref, scale_ref, q_ref, k_ref, v_ref, g_ref, dk_ref, dv_ref, k_acc, v_acc
):
    pair = pl.program_id(0)
    blocks = q_ref.shape[0] // rows
    lanes = q_ref.shape[1]
    half = lanes // 2
    first_half = lax.broadcasted_iota(jnp.int32, (rows, lanes), 1) < half
    zero = jnp.zeros((rows, lanes), jnp.bfloat16)
    col = lax.broadcasted_iota(jnp.int32, (1, 2 * rows), 1)
    scale = jnp.where(col < rows, scale_ref[2 * pair], scale_ref[2 * pair + 1])
    k_acc[...] = jnp.zeros_like(k_acc)
    v_acc[...] = jnp.zeros_like(v_acc)

    def both_heads(x):
        return jnp.concatenate([jnp.where(first_half, x, zero), jnp.where(first_half, zero, x)], 0)

    def step(b, carry):
        def tile_at(ref, block):
            return ref[pl.ds(pl.multiple_of(block * rows, rows), rows), :]

        near = [jnp.maximum(b - 1, 0), b, jnp.minimum(b + 1, blocks - 1)]
        q_two = both_heads(tile_at(q_ref, b))
        g_own = tile_at(g_ref, b)
        g_two = both_heads(g_own)
        keys = jnp.concatenate([tile_at(k_ref, c) for c in near], 0)
        values = jnp.concatenate([tile_at(v_ref, c) for c in near], 0)
        raw = nt_dot(keys, q_two)
        scores = jnp.concatenate(
            [
                jnp.where(
                    neighbors_ref[b, d] >= 0, raw[d * rows : (d + 1) * rows] * scale, NEG_FILL
                )
                for d in range(3)
            ],
            0,
        )
        row_max = jnp.max(scores, axis=0, keepdims=True)
        powers = jnp.exp(scores - row_max)
        total = jnp.sum(powers, axis=0, keepdims=True)
        weights = powers * (1.0 / total)
        weights_b = weights.astype(jnp.bfloat16)
        attended = tn_dot(values, weights_b).astype(jnp.bfloat16).astype(jnp.float32)
        g_turned = g_own.astype(jnp.float32).T
        row_dot = jnp.concatenate(
            [
                jnp.sum(g_turned[:half] * attended[:half, :rows], axis=0, keepdims=True),
                jnp.sum(g_turned[half:] * attended[half:, rows:], axis=0, keepdims=True),
            ],
            1,
        )
        dweights = nt_dot(values, g_two)
        dscores = (weights * (dweights - row_dot) * scale).astype(jnp.bfloat16)
        v_part = jnp.dot(weights_b, g_two, preferred_element_type=jnp.float32)
        k_part = jnp.dot(dscores, q_two, preferred_element_type=jnp.float32)
        at = pl.ds(pl.multiple_of(b * rows, rows), 3 * rows)
        k_acc[at, :] += k_part
        v_acc[at, :] += v_part
        return carry

    lax.fori_loop(0, blocks, step, 0, unroll=2)
    inner = pl.ds(rows, blocks * rows)
    dk_ref[...] = k_acc[inner, :].astype(jnp.bfloat16)
    dv_ref[...] = v_acc[inner, :].astype(jnp.bfloat16)


def attend(queries, keys, values, grads, neighbors, head_scale, rows):
    buses, feat = queries.shape
    heads = head_scale.shape[0]
    lanes = 2 * feat // heads
    spec = pl.BlockSpec((buses, lanes), lambda p, *_: (0, p))
    out = jax.ShapeDtypeStruct((buses, feat), jnp.bfloat16)
    return pl.pallas_call(
        functools.partial(attend_kernel, rows),
        grid_spec=pltpu.PrefetchScalarGridSpec(
            num_scalar_prefetch=2,
            grid=(heads // 2,),
            in_specs=[spec] * 4,
            out_specs=[spec, spec],
            scratch_shapes=[
                pltpu.VMEM((buses + 2 * rows, lanes), jnp.float32),
                pltpu.VMEM((buses + 2 * rows, lanes), jnp.float32),
            ],
        ),
        out_shape=[out, out],
        compiler_params=pltpu.CompilerParams(vmem_limit_bytes=48 << 20),
        cost_estimate=pl.CostEstimate(
            flops=2 * 5 * 3 * rows * buses * feat,
            bytes_accessed=2 * 6 * buses * feat,
            transcendentals=3 * rows * buses * heads,
        ),
        name="attend",
    )(neighbors, head_scale, queries, keys, values, grads)


def on_device(
    series,
    hour_ids,
    hour_table,
    norm_gain,
    bus_order,
    w_query,
    w_key,
    w_value,
    score_scale,
    neighbors,
    grad_out,
):
    head_count = score_scale.shape[0]
    snap_count, block_rows, feat_width = grad_out.shape
    own_snaps, bus_count, _ = series.shape
    devices = lax.axis_size("bus")
    head_scale = score_scale / math.sqrt(feat_width // head_count)
    grads = lax.all_to_all(grad_out, "bus", split_axis=0, concat_axis=1, tiled=True)
    results = []
    for s in range(own_snaps):
        queries, keys, values = encode(
            series[s], hour_ids[s : s + 1], hour_table, norm_gain, bus_order,
            w_query, w_key, w_value, math.gcd(bus_count, 256),
        )
        results.append(
            attend(queries, keys, values, grads[s], neighbors, head_scale, block_rows)
        )
    both = jnp.stack([jnp.stack(pieces) for pieces in zip(*results)])
    both = both.reshape(2, own_snaps, devices, block_rows, feat_width).transpose(2, 0, 1, 3, 4)
    back = lax.all_to_all(both, "bus", split_axis=0, concat_axis=0, tiled=True)
    back = back.transpose(1, 0, 2, 3, 4).reshape(2, snap_count, block_rows, feat_width)
    return (back[0], back[1])


def solution(mesh):
    return jax.shard_map(
        on_device,
        mesh=mesh,
        in_specs=(
            P(("grp", "bus"), None, None),
            P(("grp", "bus")),
            P(),
            P(),
            P("grp"),
            P(),
            P(),
            P(),
            P(),
            P("grp", None),
            P("grp", "bus", None),
        ),
        out_specs=(P("grp", "bus", None), P("grp", "bus", None)),
        check_vma=False,
    )
```

```python
import functools
import math

import jax
import jax.numpy as jnp
from jax import lax
from jax.experimental import pallas as pl
from jax.experimental.pallas import tpu as pltpu
from jax.sharding import PartitionSpec as P

EPSILON = 1e-05
NEG_FILL = -1e30
VMEM_LIMIT = 56 << 20
WEIGHT_COPIES = 1


def nt_dot(a, b):
    return lax.dot_general(a, b, (((1,), (1,)), ((), ())), preferred_element_type=jnp.float32)


def tn_dot(a, b):
    return lax.dot_general(a, b, (((0,), (0,)), ((), ())), preferred_element_type=jnp.float32)


def encode_kernel(
    hour_ref, order_ref, series_ref, table_ref, gain_ref, wq_ref, wk_ref, wv_ref, q_ref, k_ref, v_ref
):
    tile = order_ref.shape[0]
    buses = series_ref.shape[0]
    hours = table_ref.shape[0]
    pick = lax.broadcasted_iota(jnp.int32, (tile, buses), 1) == order_ref[...]
    ordered = jnp.dot(
        pick.astype(jnp.bfloat16), series_ref[...], preferred_element_type=jnp.float32
    )
    table = table_ref[...].astype(jnp.float32)
    is_hour = lax.broadcasted_iota(jnp.int32, (hours, 1), 0) == hour_ref[0]
    hour_row = jnp.sum(jnp.where(is_hour, table, 0.0), axis=0, keepdims=True)
    mixed = ordered + hour_row
    power = jnp.mean(mixed * mixed, axis=1, keepdims=True)
    normed = (mixed * lax.rsqrt(power + EPSILON) * gain_ref[...]).astype(jnp.bfloat16)
    for weight_ref, out_ref in ((wq_ref, q_ref), (wk_ref, k_ref), (wv_ref, v_ref)):
        out_ref[...] = jnp.dot(
            normed, weight_ref[...], preferred_element_type=jnp.float32
        ).astype(jnp.bfloat16)


def encode(series, hour_ids, hour_table, norm_gain, order, w_query, w_key, w_value, tile):
    buses, width = series.shape
    feat = w_query.shape[1]
    whole = lambda shape: pl.BlockSpec(shape, lambda i, *_: (0, 0))
    row_spec = pl.BlockSpec((tile, feat), lambda i, *_: (i, 0))
    out = jax.ShapeDtypeStruct((buses, feat), jnp.bfloat16)
    return pl.pallas_call(
        encode_kernel,
        grid_spec=pltpu.PrefetchScalarGridSpec(
            num_scalar_prefetch=1,
            grid=(buses // tile,),
            in_specs=[
                pl.BlockSpec((tile, 1), lambda i, *_: (i, 0)),
                whole((buses, width)),
                whole(hour_table.shape),
                whole((1, width)),
                whole((width, feat)),
                whole((width, feat)),
                whole((width, feat)),
            ],
            out_specs=[row_spec, row_spec, row_spec],
        ),
        out_shape=[out, out, out],
        compiler_params=pltpu.CompilerParams(vmem_limit_bytes=VMEM_LIMIT),
        cost_estimate=pl.CostEstimate(
            flops=2 * buses * width * (buses + 3 * feat),
            bytes_accessed=2 * (buses * width + 3 * width * feat + 3 * buses * feat),
            transcendentals=buses,
        ),
        name="encode",
    )(
        hour_ids,
        order.reshape(buses, 1),
        series,
        hour_table,
        norm_gain.reshape(1, width),
        w_query,
        w_key,
        w_value,
    )


def both_heads(x):
    first_half = lax.broadcasted_iota(jnp.int32, x.shape, 1) < x.shape[1] // 2
    zero = jnp.zeros_like(x)
    return jnp.concatenate([jnp.where(first_half, x, zero), jnp.where(first_half, zero, x)], 0)


def tile_at(ref, block, rows):
    return ref[block * rows : (block + 1) * rows, :]


def near_tiles(ref, block, rows):
    last = ref.shape[0] // rows - 1
    near = (max(block - 1, 0), block, min(block + 1, last))
    return jnp.concatenate([tile_at(ref, c, rows) for c in near], 0)


def head_scales(scale_ref, rows):
    pair = pl.program_id(0)
    col = lax.broadcasted_iota(jnp.int32, (1, 2 * rows), 1)
    return jnp.where(col < rows, scale_ref[2 * pair], scale_ref[2 * pair + 1])


def softmax_over_keys(raw, scale, neighbors_ref, block, rows):
    scale_log2 = scale * math.log2(math.e)
    read = [neighbors_ref[block, d] >= 0 for d in range(3)]
    tiles = [raw[d * rows : (d + 1) * rows] for d in range(3)]
    tops = [
        jnp.where(ok, jnp.max(tile, axis=0, keepdims=True) * scale_log2, NEG_FILL)
        for ok, tile in zip(read, tiles)
    ]
    row_max = jnp.maximum(jnp.maximum(tops[0], tops[1]), tops[2])
    powers = jnp.concatenate(
        [
            jnp.exp2(tile * scale_log2 - jnp.where(ok, row_max, -NEG_FILL))
            for ok, tile in zip(read, tiles)
        ],
        0,
    )
    return powers * (1.0 / jnp.sum(powers, axis=0, keepdims=True))


class KeySums:
    def __init__(self, out_ref, rows):
        self.out_ref, self.rows, self.open = out_ref, rows, [None, None]

    def store(self, block, value):
        self.out_ref[block * self.rows : (block + 1) * self.rows, :] = value.astype(jnp.bfloat16)

    def add(self, block, part):
        low, own, high = [part[d * self.rows : (d + 1) * self.rows] for d in range(3)]
        if block > 0:
            self.store(block - 1, self.open[0] + low)
            own = self.open[1] + own
        self.open = [own, high]

    def close(self, block):
        self.store(block, self.open[0])


def weights_kernel(rows, neighbors_ref, scale_ref, q_ref, k_ref, w_ref):
    blocks = q_ref.shape[0] // rows
    scale = head_scales(scale_ref, rows)

    def products(b):
        return nt_dot(near_tiles(k_ref, b, rows), both_heads(tile_at(q_ref, b, rows)))

    raw = products(0)
    for b in range(blocks):
        ahead = products(b + 1) if b + 1 < blocks else None
        weights = softmax_over_keys(raw, scale, neighbors_ref, b, rows)
        w_ref[0, b] = weights.astype(jnp.bfloat16)
        raw = ahead


def value_kernel(rows, *refs):
    *w_refs, g_ref, dv_ref = refs
    blocks = g_ref.shape[0] // rows
    held = w_refs[0].shape[1]
    sums = KeySums(dv_ref, rows)

    def products(b):
        g_two = both_heads(tile_at(g_ref, b, rows))
        return jnp.dot(w_refs[b // held][0, b % held], g_two, preferred_element_type=jnp.float32)

    part = products(0)
    for b in range(blocks):
        ahead = products(b + 1) if b + 1 < blocks else None
        sums.add(b, part)
        part = ahead
    sums.close(blocks - 1)


def key_kernel(rows, neighbors_ref, scale_ref, q_ref, k_ref, v_ref, g_ref, dk_ref):
    blocks = q_ref.shape[0] // rows
    half = q_ref.shape[1] // 2
    scale = head_scales(scale_ref, rows)
    sums = KeySums(dk_ref, rows)

    def products(b):
        q_two = both_heads(tile_at(q_ref, b, rows))
        g_two = both_heads(tile_at(g_ref, b, rows))
        values = near_tiles(v_ref, b, rows)
        raw = nt_dot(near_tiles(k_ref, b, rows), q_two)
        return q_two, values, raw, nt_dot(values, g_two)

    def normalise(b, found):
        q_two, values, raw, dweights = found
        weights = softmax_over_keys(raw, scale, neighbors_ref, b, rows)
        attended = tn_dot(values, weights.astype(jnp.bfloat16))
        return q_two, dweights, weights, attended.astype(jnp.bfloat16).astype(jnp.float32)

    def finish(b, found):
        q_two, dweights, weights, attended = found
        turned = tile_at(g_ref, b, rows).astype(jnp.float32).T
        row_dot = jnp.concatenate(
            [
                jnp.sum(turned[:half] * attended[:half, :rows], axis=0, keepdims=True),
                jnp.sum(turned[half:] * attended[half:, rows:], axis=0, keepdims=True),
            ],
            1,
        )
        dscores = (weights * (dweights - row_dot) * scale).astype(jnp.bfloat16)
        sums.add(b, jnp.dot(dscores, q_two, preferred_element_type=jnp.float32))

    one, two = products(0), None
    for b in range(blocks):
        ahead = products(b + 1) if b + 1 < blocks else None
        now = normalise(b, one)
        if two is not None:
            finish(b - 1, two)
        one, two = ahead, now
    finish(blocks - 1, two)
    sums.close(blocks - 1)


def copy_kernel(x_ref, out_ref):
    out_ref[...] = x_ref[...]


def copied(value):
    run = math.gcd(value.shape[0], 4)
    spec = pl.BlockSpec((value.shape[0] // run,) + value.shape[1:], lambda i: (i, 0, 0))
    return pl.pallas_call(
        copy_kernel,
        grid=(run,),
        in_specs=[spec],
        out_specs=spec,
        out_shape=jax.ShapeDtypeStruct(value.shape, value.dtype),
        compiler_params=pltpu.CompilerParams(vmem_limit_bytes=8 << 20),
        cost_estimate=pl.CostEstimate(flops=0, bytes_accessed=4 * value.size, transcendentals=0),
        name="settle",
    )(value)


def by_pair(kernel, name, rows, heads, scalars, arrays, out_shape, limit, dots, exps):
    buses, feat = arrays[-1].shape
    lanes = 2 * feat // heads
    lane_spec = pl.BlockSpec((buses, lanes), lambda p, *_: (0, p))
    whole, pieces = [], []
    for x in arrays:
        count = WEIGHT_COPIES if x.ndim > 2 else 1
        for i in range(count):
            whole.append(x)
            pieces.append(weights_spec(x.shape, count, i) if x.ndim > 2 else lane_spec)
    out_spec = weights_spec(out_shape, 1, 0) if len(out_shape) > 2 else lane_spec
    moved = sum(math.prod(x.shape) for x in arrays) + math.prod(out_shape)
    return pl.pallas_call(
        functools.partial(kernel, rows),
        grid_spec=pltpu.PrefetchScalarGridSpec(
            num_scalar_prefetch=len(scalars),
            grid=(heads // 2,),
            in_specs=pieces,
            out_specs=out_spec,
        ),
        out_shape=pltpu.HBM(out_shape, jnp.bfloat16),
        compiler_params=pltpu.CompilerParams(vmem_limit_bytes=limit),
        cost_estimate=pl.CostEstimate(
            flops=2 * dots * 3 * rows * buses * feat,
            bytes_accessed=2 * moved,
            transcendentals=exps * 3 * rows * buses * heads,
        ),
        name=name,
    )(*scalars, *whole)


def weights_spec(shape, count, at):
    return pl.BlockSpec((1, shape[1] // count) + shape[2:], lambda p, *_: (p, at, 0, 0))


def on_device(
    series,
    hour_ids,
    hour_table,
    norm_gain,
    bus_order,
    w_query,
    w_key,
    w_value,
    score_scale,
    neighbors,
    grad_out,
):
    head_count = score_scale.shape[0]
    snap_count, block_rows, feat_width = grad_out.shape
    own_snaps, bus_count, _ = series.shape
    devices = lax.axis_size("bus")
    head_scale = score_scale / math.sqrt(feat_width // head_count)

    def exchange(value):
        return lax.all_to_all(value, "bus", split_axis=0, concat_axis=0, tiled=True)

    def give_back(pieces):
        value = jnp.stack([piece.reshape(devices, block_rows, feat_width) for piece in pieces], 1)
        return exchange(value).reshape(snap_count, block_rows, feat_width)

    grads = exchange(grad_out.reshape(devices, own_snaps, block_rows, feat_width))
    scalars = (neighbors, head_scale)
    shape = (bus_count, feat_width)
    weight_shape = (head_count // 2, bus_count // block_rows, 3 * block_rows, 2 * block_rows)
    value_grads, key_grads = [], []
    for s in range(own_snaps):
        queries, keys, values = encode(
            series[s], hour_ids[s : s + 1], hour_table, norm_gain, bus_order,
            w_query, w_key, w_value, math.gcd(bus_count, 256),
        )
        weights = by_pair(
            weights_kernel, "weights", block_rows, head_count, scalars, (queries, keys),
            weight_shape, VMEM_LIMIT, 1, 1,
        )
        own_grads = grads[:, s].reshape(shape)
        value_grads.append(
            by_pair(
                value_kernel, "value_grad", block_rows, head_count, (),
                (weights, own_grads),
                shape, 52 << 20, 1, 0,
            )
        )
        own_grads, _ = lax.optimization_barrier((own_grads, value_grads[-1]))
        key_grads.append(
            by_pair(
                key_kernel, "key_grad", block_rows, head_count, scalars,
                (queries, keys, values, own_grads), shape, VMEM_LIMIT, 4, 1,
            )
        )
    value_grad = give_back(value_grads)
    value_grad, key_grads = lax.optimization_barrier((value_grad, key_grads))
    key_grad = give_back(key_grads)
    return (key_grad, copied(value_grad))


def solution(mesh):
    return jax.shard_map(
        on_device,
        mesh=mesh,
        in_specs=(
            P(("grp", "bus"), None, None),
            P(("grp", "bus")),
            P(),
            P(),
            P("grp"),
            P(),
            P(),
            P(),
            P(),
            P("grp", None),
            P("grp", "bus", None),
        ),
        out_specs=(P("grp", "bus", None), P("grp", "bus", None)),
        check_vma=False,
    )
```

```python
import functools
import math

import jax
import jax.numpy as jnp
from jax import lax
from jax.experimental import pallas as pl
from jax.experimental.pallas import tpu as pltpu
from jax.sharding import PartitionSpec as P

EPSILON = 1e-05
NEG_FILL = -1e30
VMEM_LIMIT = 56 << 20
SETTLE_STEPS = 4
EARLY_PAIRS = 2
PLANE = 4


def nt_dot(a, b):
    return lax.dot_general(a, b, (((1,), (1,)), ((), ())), preferred_element_type=jnp.float32)


def tn_dot(a, b):
    return lax.dot_general(a, b, (((0,), (0,)), ((), ())), preferred_element_type=jnp.float32)


def encode_kernel(
    hour_ref, order_ref, series_ref, table_ref, gain_ref, wq_ref, wk_ref, wv_ref, q_ref, k_ref, v_ref
):
    tile = order_ref.shape[0]
    buses = series_ref.shape[0]
    hours = table_ref.shape[0]
    pick = lax.broadcasted_iota(jnp.int32, (tile, buses), 1) == order_ref[...]
    ordered = jnp.dot(
        pick.astype(jnp.bfloat16), series_ref[...], preferred_element_type=jnp.float32
    )
    table = table_ref[...].astype(jnp.float32)
    is_hour = lax.broadcasted_iota(jnp.int32, (hours, 1), 0) == hour_ref[0]
    hour_row = jnp.sum(jnp.where(is_hour, table, 0.0), axis=0, keepdims=True)
    mixed = ordered + hour_row
    power = jnp.mean(mixed * mixed, axis=1, keepdims=True)
    normed = (mixed * lax.rsqrt(power + EPSILON) * gain_ref[...]).astype(jnp.bfloat16)
    for weight_ref, out_ref in ((wq_ref, q_ref), (wk_ref, k_ref), (wv_ref, v_ref)):
        out_ref[...] = jnp.dot(
            normed, weight_ref[...], preferred_element_type=jnp.float32
        ).astype(jnp.bfloat16)


def encode(series, hour_ids, hour_table, norm_gain, order, w_query, w_key, w_value, tile):
    buses, width = series.shape
    feat = w_query.shape[1]
    whole = lambda shape: pl.BlockSpec(shape, lambda i, *_: (0, 0))
    row_spec = pl.BlockSpec((tile, feat), lambda i, *_: (i, 0))
    out = jax.ShapeDtypeStruct((buses, feat), jnp.bfloat16)
    return pl.pallas_call(
        encode_kernel,
        grid_spec=pltpu.PrefetchScalarGridSpec(
            num_scalar_prefetch=1,
            grid=(buses // tile,),
            in_specs=[
                pl.BlockSpec((tile, 1), lambda i, *_: (i, 0)),
                whole((buses, width)),
                whole(hour_table.shape),
                whole((1, width)),
                whole((width, feat)),
                whole((width, feat)),
                whole((width, feat)),
            ],
            out_specs=[row_spec, row_spec, row_spec],
        ),
        out_shape=[out, out, out],
        compiler_params=pltpu.CompilerParams(vmem_limit_bytes=VMEM_LIMIT),
        cost_estimate=pl.CostEstimate(
            flops=2 * buses * width * (buses + 3 * feat),
            bytes_accessed=2 * (buses * width + 3 * width * feat + 3 * buses * feat),
            transcendentals=buses,
        ),
        name="encode",
    )(
        hour_ids,
        order.reshape(buses, 1),
        series,
        hour_table,
        norm_gain.reshape(1, width),
        w_query,
        w_key,
        w_value,
    )


def both_heads(x):
    first_half = lax.broadcasted_iota(jnp.int32, x.shape, 1) < x.shape[1] // 2
    zero = jnp.zeros_like(x)
    return jnp.concatenate([jnp.where(first_half, x, zero), jnp.where(first_half, zero, x)], 0)


def tile_at(ref, block, rows):
    return ref[block * rows : (block + 1) * rows, :]


def near_tiles(ref, block, rows):
    last = ref.shape[0] // rows - 1
    near = (max(block - 1, 0), block, min(block + 1, last))
    return jnp.concatenate([tile_at(ref, c, rows) for c in near], 0)


def head_scales(scale_ref, rows):
    pair = pl.program_id(0)
    col = lax.broadcasted_iota(jnp.int32, (1, 2 * rows), 1)
    return jnp.where(col < rows, scale_ref[2 * pair], scale_ref[2 * pair + 1])


def softmax_over_keys(raw, scale, neighbors_ref, block, rows):
    scale_log2 = scale * math.log2(math.e)
    read = [neighbors_ref[block, d] >= 0 for d in range(3)]
    tiles = [raw[d * rows : (d + 1) * rows] for d in range(3)]
    tops = [
        jnp.where(ok, jnp.max(tile, axis=0, keepdims=True) * scale_log2, NEG_FILL)
        for ok, tile in zip(read, tiles)
    ]
    row_max = jnp.maximum(jnp.maximum(tops[0], tops[1]), tops[2])
    powers = jnp.concatenate(
        [
            jnp.exp2(tile * scale_log2 - jnp.where(ok, row_max, -NEG_FILL))
            for ok, tile in zip(read, tiles)
        ],
        0,
    )
    total = jnp.sum(powers, axis=0, keepdims=True)
    return powers * (1.0 / total), row_max + jnp.log2(total)


class KeySums:
    def __init__(self, out_ref, rows, flip=None):
        self.out_ref, self.rows, self.flip, self.open = out_ref, rows, flip, [None, None]

    def store(self, block, value):
        start = block * self.rows
        if self.flip is not None:
            start = pl.multiple_of((self.flip ^ block) * self.rows, self.rows)
        self.out_ref[pl.ds(start, self.rows), :] = value.astype(jnp.bfloat16)

    def add(self, block, part):
        low, own, high = [part[d * self.rows : (d + 1) * self.rows] for d in range(3)]
        if block > 0:
            self.store(block - 1, self.open[0] + low)
            own = self.open[1] + own
        self.open = [own, high]

    def close(self, block):
        self.store(block, self.open[0])


def weights_kernel(
    rows, neighbors_ref, scale_ref, q_ref, k_ref, v_ref, w_ref, attended_ref, shift_ref
):
    blocks = q_ref.shape[0] // rows
    scale = head_scales(scale_ref, rows)

    def products(b):
        return nt_dot(near_tiles(k_ref, b, rows), both_heads(tile_at(q_ref, b, rows)))

    def attend(b, weights_b):
        attended = tn_dot(near_tiles(v_ref, b, rows), weights_b)
        attended_ref[0, b] = attended.astype(jnp.bfloat16)

    raw, last = products(0), None
    for b in range(blocks):
        ahead = products(b + 1) if b + 1 < blocks else None
        weights, shift = softmax_over_keys(raw, scale, neighbors_ref, b, rows)
        weights_b = weights.astype(jnp.bfloat16)
        w_ref[0, b] = weights_b
        shift_ref[0, b : b + 1] = shift
        if last is not None:
            attend(b - 1, last)
        raw, last = ahead, weights_b
    attend(blocks - 1, last)


def flipped_value_kernel(rows, me_ref, *refs):
    value_kernel(rows, *refs, flip=me_ref[0])


def value_kernel(rows, w_ref, g_ref, *rest, flip=None):
    dv_ref = rest[-1]
    blocks = g_ref.shape[0] // rows
    sums = KeySums(dv_ref, rows, flip)

    def products(b):
        g_two = both_heads(tile_at(g_ref, b, rows))
        return jnp.dot(w_ref[0, b], g_two, preferred_element_type=jnp.float32)

    part = products(0)
    for b in range(blocks):
        ahead = products(b + 1) if b + 1 < blocks else None
        sums.add(b, part)
        part = ahead
    sums.close(blocks - 1)


def key_kernel(
    rows, neighbors_ref, scale_ref, q_ref, k_ref, v_ref, g_ref, attended_ref, shift_ref, *rest
):
    dk_ref = rest[-1]
    blocks = q_ref.shape[0] // rows
    half = q_ref.shape[1] // 2
    scale = head_scales(scale_ref, rows)
    scale_log2 = scale * math.log2(math.e)
    sums = KeySums(dk_ref, rows)

    def products(b):
        q_two = both_heads(tile_at(q_ref, b, rows))
        g_two = both_heads(tile_at(g_ref, b, rows))
        raw = nt_dot(near_tiles(k_ref, b, rows), q_two)
        return q_two, raw, nt_dot(near_tiles(v_ref, b, rows), g_two)

    def finish(b, found):
        q_two, raw, dweights = found
        shift = shift_ref[0, b : b + 1]
        weights = jnp.concatenate(
            [
                jnp.exp2(
                    raw[d * rows : (d + 1) * rows] * scale_log2
                    - jnp.where(neighbors_ref[b, d] >= 0, shift, -NEG_FILL)
                )
                for d in range(3)
            ],
            0,
        )
        turned = tile_at(g_ref, b, rows).astype(jnp.float32).T
        attended = attended_ref[0, b].astype(jnp.float32)
        row_dot = jnp.concatenate(
            [
                jnp.sum(turned[:half] * attended[:half, :rows], axis=0, keepdims=True),
                jnp.sum(turned[half:] * attended[half:, rows:], axis=0, keepdims=True),
            ],
            1,
        )
        dscores = (weights * (dweights - row_dot) * scale).astype(jnp.bfloat16)
        return jnp.dot(dscores, q_two, preferred_element_type=jnp.float32)

    one, part = products(0), None
    for b in range(blocks):
        ahead = products(b + 1) if b + 1 < blocks else None
        now = finish(b, one)
        if part is not None:
            sums.add(b - 1, part)
        one, part = ahead, now
    sums.add(blocks - 1, part)
    sums.close(blocks - 1)


def settle_kernel(me_ref, x_ref, out_ref):
    out_ref[...] = x_ref[...]


def settle(me, swapped, feat):
    devices, rows, lanes = swapped.shape
    block = (1, rows, lanes)
    return pl.pallas_call(
        settle_kernel,
        grid_spec=pltpu.PrefetchScalarGridSpec(
            num_scalar_prefetch=1,
            grid=(devices,),
            in_specs=[pl.BlockSpec(block, lambda j, me_ref: (j, 0, 0))],
            out_specs=pl.BlockSpec(block, lambda j, me_ref: (me_ref[0] ^ j, 0, 0)),
        ),
        out_shape=pltpu.HBM((devices, rows, feat), jnp.bfloat16),
        compiler_params=pltpu.CompilerParams(vmem_limit_bytes=8 << 20),
        cost_estimate=pl.CostEstimate(flops=0, bytes_accessed=4 * swapped.size, transcendentals=0),
        name="settle",
    )(me, swapped)


def swap(value, bits):
    devices = lax.axis_size("bus")
    return lax.ppermute(value, "bus", [(i, i ^ bits) for i in range(devices)])


def swap_far(parts):
    devices = parts.shape[0]
    planes = devices // PLANE

    far = [parts[:PLANE]]
    far += [swap(parts[PLANE * k : PLANE * (k + 1)], PLANE * k) for k in range(1, planes)]
    return far


def swap_near(far):
    planes = len(far)
    up = swap(jnp.stack([entry[2:] for entry in far]), 2)
    right = swap(jnp.stack([jnp.stack([entry[1] for entry in far]), up[:, 1]], 1), 1)
    order = []
    for k in range(planes):
        order += [far[k][0], right[k, 0], up[k, 0], right[k, 1]]
    return jnp.stack(order)


def part_kernel(late_ref, _, dk_ref, dv_ref):
    lanes = dv_ref.shape[2]
    dv_ref[...] = late_ref[:, :, :lanes]
    dk_ref[...] = late_ref[:, :, lanes:]


def part(late, settled):
    devices, rows, feat = settled.shape
    width = late.shape[2]
    run = devices // math.gcd(devices, SETTLE_STEPS)
    out = pltpu.HBM(settled.shape, jnp.bfloat16)
    whole = pl.BlockSpec((run, rows, feat), lambda i: (i, 0, 0))
    last = (2 * feat - width) // (width - feat)
    return pl.pallas_call(
        part_kernel,
        grid=(devices // run,),
        in_specs=[
            pl.BlockSpec((run, rows, width), lambda i: (i, 0, 0)),
            pl.BlockSpec(memory_space=pl.ANY),
        ],
        out_specs=[whole, pl.BlockSpec((run, rows, width - feat), lambda i: (i, 0, last))],
        out_shape=[out, out],
        input_output_aliases={1: 1},
        compiler_params=pltpu.CompilerParams(vmem_limit_bytes=24 << 20),
        cost_estimate=pl.CostEstimate(flops=0, bytes_accessed=4 * late.size, transcendentals=0),
        name="part",
    )(late, settled)


def by_pair(
    kernel, name, rows, heads, feat, first, count, scalars, arrays, outs, out_first, dots, exps,
    into=None, limit=50,
):
    buses, lanes = arrays[1].shape[0], 2 * feat // heads

    def spec(shape, at):
        if len(shape) > 2:
            zeros = (0,) * (len(shape) - 1)
            return pl.BlockSpec((1,) + shape[1:], lambda p, *_: (at + p, *zeros))
        return pl.BlockSpec((buses, lanes), lambda p, *_: (0, at + p))

    specs = [spec(x.shape, first) for x in arrays]
    arrays, alias = list(arrays), {}
    if into is not None:
        alias = {len(scalars) + len(arrays): 0}
        specs.append(pl.BlockSpec(memory_space=pl.ANY))
        arrays.append(into)
    return pl.pallas_call(
        functools.partial(kernel, rows),
        grid_spec=pltpu.PrefetchScalarGridSpec(
            num_scalar_prefetch=len(scalars),
            grid=(count,),
            in_specs=specs,
            out_specs=[spec(x.shape, out_first) for x in outs],
        ),
        out_shape=[pltpu.HBM(x.shape, x.dtype) for x in outs],
        input_output_aliases=alias,
        compiler_params=pltpu.CompilerParams(vmem_limit_bytes=limit << 20),
        cost_estimate=pl.CostEstimate(
            flops=2 * dots * 3 * rows * buses * count * lanes,
            bytes_accessed=2 * count * heads // 2 * sum(math.prod(x.shape) for x in arrays),
            transcendentals=exps * 3 * rows * buses * 2 * count,
        ),
        name=name,
    )(*scalars, *arrays)


def on_device(
    series,
    hour_ids,
    hour_table,
    norm_gain,
    bus_order,
    w_query,
    w_key,
    w_value,
    score_scale,
    neighbors,
    grad_out,
):
    head_count = score_scale.shape[0]
    snap_count, block_rows, feat_width = grad_out.shape
    bus_count = series.shape[1]
    devices = lax.axis_size("bus")
    head_scale = score_scale / math.sqrt(feat_width // head_count)
    pairs, lanes = head_count // 2, 2 * feat_width // head_count
    early = EARLY_PAIRS
    me = lax.axis_index("bus").astype(jnp.int32).reshape(1)
    late = pairs - early

    def exchange(value):
        return lax.all_to_all(value, "bus", split_axis=0, concat_axis=0, tiled=True)

    def blocks_of(value):
        return value.reshape(devices, block_rows, value.shape[-1])

    scalars = (neighbors, head_scale)
    bus_blocks = bus_count // block_rows
    bf16 = lambda *shape: jax.ShapeDtypeStruct(shape, jnp.bfloat16)
    call = functools.partial(by_pair, rows=block_rows, heads=head_count, feat=feat_width)

    grads = exchange(grad_out).reshape(bus_count, feat_width)
    queries, keys, values = encode(
        series[0], hour_ids, hour_table, norm_gain, bus_order,
        w_query, w_key, w_value, math.gcd(bus_count, 256),
    )
    weights, attended, shifts = call(
        weights_kernel, "weights", limit=56, first=0, count=pairs, scalars=scalars,
        arrays=(queries, keys, values), out_first=0, dots=2, exps=1,
        outs=[
            bf16(pairs, bus_blocks, 3 * block_rows, 2 * block_rows),
            bf16(pairs, bus_blocks, lanes, 2 * block_rows),
            jax.ShapeDtypeStruct((pairs, bus_blocks, 2 * block_rows), jnp.float32),
        ],
    )
    (early_value,) = call(
        flipped_value_kernel, "value_early", first=0, count=early, scalars=(me,),
        arrays=(weights, grads), outs=[bf16(bus_count, early * lanes)], out_first=0,
        dots=1, exps=0,
    )
    early_far = swap_far(blocks_of(early_value))
    grads, _ = lax.optimization_barrier((grads, early_value))
    rest_out = bf16(bus_count, late * lanes + feat_width)
    (rest,) = call(
        value_kernel, "value_late", first=early, count=late, scalars=(),
        arrays=(weights, grads), outs=[rest_out], out_first=0, dots=1, exps=0,
    )
    (rest,) = call(
        key_kernel, "key", first=0, count=pairs, scalars=scalars,
        arrays=(queries, keys, values, grads, attended, shifts), outs=[rest_out],
        out_first=late, dots=3, exps=1, into=rest,
    )
    early_far, rest = lax.optimization_barrier((early_far, rest))
    late_out = exchange(blocks_of(rest))
    early_out = swap_near(early_far)
    return tuple(part(late_out, settle(me, early_out, feat_width)))


def solution(mesh):
    return jax.shard_map(
        on_device,
        mesh=mesh,
        in_specs=(
            P(("grp", "bus"), None, None),
            P(("grp", "bus")),
            P(),
            P(),
            P("grp"),
            P(),
            P(),
            P(),
            P(),
            P("grp", None),
            P("grp", "bus", None),
        ),
        out_specs=(P("grp", "bus", None), P("grp", "bus", None)),
        check_vma=False,
    )
```

```python
import functools
import math

import jax
import jax.numpy as jnp
from jax import lax
from jax.experimental import pallas as pl
from jax.experimental.pallas import tpu as pltpu
from jax.sharding import PartitionSpec as P

EPSILON = 1e-05
NEG_FILL = -1e30
VMEM_LIMIT = 56 << 20
SETTLE_STEPS = 2
EARLY_PAIRS = 2
PLANE = 4


def nt_dot(a, b):
    return lax.dot_general(a, b, (((1,), (1,)), ((), ())), preferred_element_type=jnp.float32)


def tn_dot(a, b):
    return lax.dot_general(a, b, (((0,), (0,)), ((), ())), preferred_element_type=jnp.float32)


def encode_kernel(
    hour_ref, order_ref, series_ref, table_ref, gain_ref, wq_ref, wk_ref, wv_ref, q_ref, k_ref, v_ref
):
    tile = order_ref.shape[0]
    buses = series_ref.shape[0]
    hours = table_ref.shape[0]
    pick = lax.broadcasted_iota(jnp.int32, (tile, buses), 1) == order_ref[...]
    ordered = jnp.dot(
        pick.astype(jnp.bfloat16), series_ref[...], preferred_element_type=jnp.float32
    )
    table = table_ref[...].astype(jnp.float32)
    is_hour = lax.broadcasted_iota(jnp.int32, (hours, 1), 0) == hour_ref[0]
    hour_row = jnp.sum(jnp.where(is_hour, table, 0.0), axis=0, keepdims=True)
    mixed = ordered + hour_row
    power = jnp.mean(mixed * mixed, axis=1, keepdims=True)
    normed = (mixed * lax.rsqrt(power + EPSILON) * gain_ref[...]).astype(jnp.bfloat16)
    for weight_ref, out_ref in ((wq_ref, q_ref), (wk_ref, k_ref), (wv_ref, v_ref)):
        out_ref[...] = jnp.dot(
            normed, weight_ref[...], preferred_element_type=jnp.float32
        ).astype(jnp.bfloat16)


def encode(series, hour_ids, hour_table, norm_gain, order, w_query, w_key, w_value, tile):
    buses, width = series.shape
    feat = w_query.shape[1]
    whole = lambda shape: pl.BlockSpec(shape, lambda i, *_: (0, 0))
    row_spec = pl.BlockSpec((tile, feat), lambda i, *_: (i, 0))
    out = jax.ShapeDtypeStruct((buses, feat), jnp.bfloat16)
    return pl.pallas_call(
        encode_kernel,
        grid_spec=pltpu.PrefetchScalarGridSpec(
            num_scalar_prefetch=1,
            grid=(buses // tile,),
            in_specs=[
                pl.BlockSpec((tile, 1), lambda i, *_: (i, 0)),
                whole((buses, width)),
                whole(hour_table.shape),
                whole((1, width)),
                whole((width, feat)),
                whole((width, feat)),
                whole((width, feat)),
            ],
            out_specs=[row_spec, row_spec, row_spec],
        ),
        out_shape=[out, out, out],
        compiler_params=pltpu.CompilerParams(vmem_limit_bytes=VMEM_LIMIT),
        cost_estimate=pl.CostEstimate(
            flops=2 * buses * width * (buses + 3 * feat),
            bytes_accessed=2 * (buses * width + 3 * width * feat + 3 * buses * feat),
            transcendentals=buses,
        ),
        name="encode",
    )(
        hour_ids,
        order.reshape(buses, 1),
        series,
        hour_table,
        norm_gain.reshape(1, width),
        w_query,
        w_key,
        w_value,
    )


def both_heads(x):
    first_half = lax.broadcasted_iota(jnp.int32, x.shape, 1) < x.shape[1] // 2
    zero = jnp.zeros_like(x)
    return jnp.concatenate([jnp.where(first_half, x, zero), jnp.where(first_half, zero, x)], 0)


def tile_at(ref, block, rows):
    return ref[block * rows : (block + 1) * rows, :]


def near_tiles(ref, block, rows):
    last = ref.shape[0] // rows - 1
    near = (max(block - 1, 0), block, min(block + 1, last))
    return jnp.concatenate([tile_at(ref, c, rows) for c in near], 0)


def head_scales(scale_ref, rows):
    pair = pl.program_id(0)
    col = lax.broadcasted_iota(jnp.int32, (1, 2 * rows), 1)
    return jnp.where(col < rows, scale_ref[2 * pair], scale_ref[2 * pair + 1])


def softmax_over_keys(raw, scale, neighbors_ref, block, rows):
    scale_log2 = scale * math.log2(math.e)
    read = [neighbors_ref[block, d] >= 0 for d in range(3)]
    tiles = [raw[d * rows : (d + 1) * rows] for d in range(3)]
    tops = [
        jnp.where(ok, jnp.max(tile, axis=0, keepdims=True) * scale_log2, NEG_FILL)
        for ok, tile in zip(read, tiles)
    ]
    row_max = jnp.maximum(jnp.maximum(tops[0], tops[1]), tops[2])
    powers = jnp.concatenate(
        [
            jnp.exp2(tile * scale_log2 - jnp.where(ok, row_max, -NEG_FILL))
            for ok, tile in zip(read, tiles)
        ],
        0,
    )
    total = jnp.sum(powers, axis=0, keepdims=True)
    return powers * (1.0 / total), row_max + jnp.log2(total)


class KeySums:
    def __init__(self, out_ref, rows):
        self.out_ref, self.rows, self.open = out_ref, rows, [None, None]

    def store(self, block, value):
        self.out_ref[block * self.rows : (block + 1) * self.rows, :] = value.astype(jnp.bfloat16)

    def add(self, block, part):
        low, own, high = [part[d * self.rows : (d + 1) * self.rows] for d in range(3)]
        if block > 0:
            self.store(block - 1, self.open[0] + low)
            own = self.open[1] + own
        self.open = [own, high]

    def close(self, block):
        self.store(block, self.open[0])


def weights_kernel(
    rows, neighbors_ref, scale_ref, q_ref, k_ref, v_ref, w_ref, attended_ref, shift_ref
):
    blocks = q_ref.shape[0] // rows
    scale = head_scales(scale_ref, rows)

    def products(b):
        return nt_dot(near_tiles(k_ref, b, rows), both_heads(tile_at(q_ref, b, rows)))

    def attend(b, weights_b):
        attended = tn_dot(near_tiles(v_ref, b, rows), weights_b)
        attended_ref[0, b] = attended.astype(jnp.bfloat16)

    raw, last = products(0), None
    for b in range(blocks):
        ahead = products(b + 1) if b + 1 < blocks else None
        weights, shift = softmax_over_keys(raw, scale, neighbors_ref, b, rows)
        weights_b = weights.astype(jnp.bfloat16)
        w_ref[0, b] = weights_b
        shift_ref[0, b : b + 1] = shift
        if last is not None:
            attend(b - 1, last)
        raw, last = ahead, weights_b
    attend(blocks - 1, last)


def early_value_kernel(rows, me_ref, w_ref, g_ref, *rest):
    *outs, held = rest
    value_kernel(rows, w_ref, g_ref, held)
    for k, out in enumerate(outs):
        for i in range(PLANE):
            block = me_ref[0] ^ (PLANE * k + i)
            tile = held[pl.ds(pl.multiple_of(block * rows, rows), rows), :]
            out[i * rows : (i + 1) * rows, :] = tile


def value_kernel(rows, w_ref, g_ref, *rest):
    dv_ref = rest[-1]
    blocks = g_ref.shape[0] // rows
    sums = KeySums(dv_ref, rows)

    def products(b):
        g_two = both_heads(tile_at(g_ref, b, rows))
        return jnp.dot(w_ref[0, b], g_two, preferred_element_type=jnp.float32)

    part = products(0)
    for b in range(blocks):
        ahead = products(b + 1) if b + 1 < blocks else None
        sums.add(b, part)
        part = ahead
    sums.close(blocks - 1)


def key_kernel(
    rows, neighbors_ref, scale_ref, q_ref, k_ref, v_ref, g_ref, attended_ref, shift_ref, *rest
):
    dk_ref = rest[-1]
    blocks = q_ref.shape[0] // rows
    half = q_ref.shape[1] // 2
    scale = head_scales(scale_ref, rows)
    scale_log2 = scale * math.log2(math.e)
    sums = KeySums(dk_ref, rows)

    def products(b):
        q_two = both_heads(tile_at(q_ref, b, rows))
        g_two = both_heads(tile_at(g_ref, b, rows))
        raw = nt_dot(near_tiles(k_ref, b, rows), q_two)
        return q_two, raw, nt_dot(near_tiles(v_ref, b, rows), g_two)

    def finish(b, found):
        q_two, raw, dweights = found
        shift = shift_ref[0, b : b + 1]
        weights = jnp.concatenate(
            [
                jnp.exp2(
                    raw[d * rows : (d + 1) * rows] * scale_log2
                    - jnp.where(neighbors_ref[b, d] >= 0, shift, -NEG_FILL)
                )
                for d in range(3)
            ],
            0,
        )
        turned = tile_at(g_ref, b, rows).astype(jnp.float32).T
        attended = attended_ref[0, b].astype(jnp.float32)
        row_dot = jnp.concatenate(
            [
                jnp.sum(turned[:half] * attended[:half, :rows], axis=0, keepdims=True),
                jnp.sum(turned[half:] * attended[half:, rows:], axis=0, keepdims=True),
            ],
            1,
        )
        dscores = (weights * (dweights - row_dot) * scale).astype(jnp.bfloat16)
        return jnp.dot(dscores, q_two, preferred_element_type=jnp.float32)

    one, part = products(0), None
    for b in range(blocks):
        ahead = products(b + 1) if b + 1 < blocks else None
        now = finish(b, one)
        if part is not None:
            sums.add(b - 1, part)
        one, part = ahead, now
    sums.add(blocks - 1, part)
    sums.close(blocks - 1)


def settle_kernel(me_ref, x_ref, out_ref):
    out_ref[...] = x_ref[...]


def settle(me, swapped, feat):
    devices, rows, lanes = swapped.shape
    block = (1, rows, lanes)
    return pl.pallas_call(
        settle_kernel,
        grid_spec=pltpu.PrefetchScalarGridSpec(
            num_scalar_prefetch=1,
            grid=(devices,),
            in_specs=[pl.BlockSpec(block, lambda j, me_ref: (j, 0, 0))],
            out_specs=pl.BlockSpec(block, lambda j, me_ref: (me_ref[0] ^ j, 0, 0)),
        ),
        out_shape=pltpu.HBM((devices, rows, feat), jnp.bfloat16),
        compiler_params=pltpu.CompilerParams(vmem_limit_bytes=8 << 20),
        cost_estimate=pl.CostEstimate(flops=0, bytes_accessed=4 * swapped.size, transcendentals=0),
        name="settle",
    )(me, swapped)


def swap(value, bits):
    devices = lax.axis_size("bus")
    return lax.ppermute(value, "bus", [(i, i ^ bits) for i in range(devices)])


def swap_far(parts):
    return [parts[0]] + [swap(part, PLANE * k) for k, part in enumerate(parts) if k]


def swap_near(far):
    planes = len(far)
    up = swap(jnp.stack([entry[2:] for entry in far]), 2)
    right = swap(jnp.stack([jnp.stack([entry[1] for entry in far]), up[:, 1]], 1), 1)
    order = []
    for k in range(planes):
        order += [far[k][0], right[k, 0], up[k, 0], right[k, 1]]
    return jnp.stack(order)


def part_kernel(late_ref, _, dk_ref, dv_ref):
    lanes = dv_ref.shape[2]
    dv_ref[...] = late_ref[:, :, :lanes]
    dk_ref[...] = late_ref[:, :, lanes:]


def part(late, settled):
    devices, rows, feat = settled.shape
    width = late.shape[2]
    run = devices // math.gcd(devices, SETTLE_STEPS)
    out = pltpu.HBM(settled.shape, jnp.bfloat16)
    whole = pl.BlockSpec((run, rows, feat), lambda i: (i, 0, 0))
    last = (2 * feat - width) // (width - feat)
    return pl.pallas_call(
        part_kernel,
        grid=(devices // run,),
        in_specs=[
            pl.BlockSpec((run, rows, width), lambda i: (i, 0, 0)),
            pl.BlockSpec(memory_space=pl.ANY),
        ],
        out_specs=[whole, pl.BlockSpec((run, rows, width - feat), lambda i: (i, 0, last))],
        out_shape=[out, out],
        input_output_aliases={1: 1},
        compiler_params=pltpu.CompilerParams(vmem_limit_bytes=24 << 20),
        cost_estimate=pl.CostEstimate(flops=0, bytes_accessed=4 * late.size, transcendentals=0),
        name="part",
    )(late, settled)


def by_pair(
    kernel, name, rows, heads, feat, first, count, scalars, arrays, outs, out_first, dots, exps,
    into=None, limit=50, scratch=(),
):
    buses, lanes = arrays[1].shape[0], 2 * feat // heads

    def spec(shape, at):
        if len(shape) > 2:
            zeros = (0,) * (len(shape) - 1)
            return pl.BlockSpec((1,) + shape[1:], lambda p, *_: (at + p, *zeros))
        return pl.BlockSpec((shape[0], lanes), lambda p, *_: (0, at + p))

    specs = [spec(x.shape, first) for x in arrays]
    arrays, alias = list(arrays), {}
    if into is not None:
        alias = {len(scalars) + len(arrays): 0}
        specs.append(pl.BlockSpec(memory_space=pl.ANY))
        arrays.append(into)
    return pl.pallas_call(
        functools.partial(kernel, rows),
        grid_spec=pltpu.PrefetchScalarGridSpec(
            num_scalar_prefetch=len(scalars),
            grid=(count,),
            in_specs=specs,
            out_specs=[spec(x.shape, out_first) for x in outs],
            scratch_shapes=scratch,
        ),
        out_shape=[pltpu.HBM(x.shape, x.dtype) for x in outs],
        input_output_aliases=alias,
        compiler_params=pltpu.CompilerParams(vmem_limit_bytes=limit << 20),
        cost_estimate=pl.CostEstimate(
            flops=2 * dots * 3 * rows * buses * count * lanes,
            bytes_accessed=2 * count * heads // 2 * sum(math.prod(x.shape) for x in arrays),
            transcendentals=exps * 3 * rows * buses * 2 * count,
        ),
        name=name,
    )(*scalars, *arrays)


def on_device(
    series,
    hour_ids,
    hour_table,
    norm_gain,
    bus_order,
    w_query,
    w_key,
    w_value,
    score_scale,
    neighbors,
    grad_out,
):
    head_count = score_scale.shape[0]
    snap_count, block_rows, feat_width = grad_out.shape
    bus_count = series.shape[1]
    devices = lax.axis_size("bus")
    head_scale = score_scale / math.sqrt(feat_width // head_count)
    pairs, lanes = head_count // 2, 2 * feat_width // head_count
    early = EARLY_PAIRS
    me = lax.axis_index("bus").astype(jnp.int32).reshape(1)
    late = pairs - early

    def exchange(value):
        return lax.all_to_all(value, "bus", split_axis=0, concat_axis=0, tiled=True)

    def blocks_of(value):
        return value.reshape(devices, block_rows, value.shape[-1])

    scalars = (neighbors, head_scale)
    bus_blocks = bus_count // block_rows
    bf16 = lambda *shape: jax.ShapeDtypeStruct(shape, jnp.bfloat16)
    call = functools.partial(by_pair, rows=block_rows, heads=head_count, feat=feat_width)

    grads = exchange(grad_out).reshape(bus_count, feat_width)
    queries, keys, values = encode(
        series[0], hour_ids, hour_table, norm_gain, bus_order,
        w_query, w_key, w_value, math.gcd(bus_count, 256),
    )
    weights, attended, shifts = call(
        weights_kernel, "weights", limit=56, first=0, count=pairs, scalars=scalars,
        arrays=(queries, keys, values), out_first=0, dots=2, exps=1,
        outs=[
            bf16(pairs, bus_blocks, 3 * block_rows, 2 * block_rows),
            bf16(pairs, bus_blocks, lanes, 2 * block_rows),
            jax.ShapeDtypeStruct((pairs, bus_blocks, 2 * block_rows), jnp.float32),
        ],
    )
    early_value = call(
        early_value_kernel, "value_early", first=0, count=early, scalars=(me,),
        arrays=(weights, grads), out_first=0, dots=1, exps=0,
        outs=[bf16(PLANE * block_rows, early * lanes)] * (devices // PLANE),
        scratch=[pltpu.VMEM((bus_count, lanes), jnp.bfloat16)],
    )
    early_far = swap_far(
        [x.reshape(PLANE, block_rows, early * lanes) for x in early_value]
    )
    grads, _ = lax.optimization_barrier((grads, early_value))
    rest_out = bf16(bus_count, late * lanes + feat_width)
    (rest,) = call(
        value_kernel, "value_late", first=early, count=late, scalars=(),
        arrays=(weights, grads), outs=[rest_out], out_first=0, dots=1, exps=0,
    )
    (rest,) = call(
        key_kernel, "key", first=0, count=pairs, scalars=scalars,
        arrays=(queries, keys, values, grads, attended, shifts), outs=[rest_out],
        out_first=late, dots=3, exps=1, into=rest,
    )
    early_far, rest = lax.optimization_barrier((early_far, rest))
    late_out = exchange(blocks_of(rest))
    early_out = swap_near(early_far)
    return tuple(part(late_out, settle(me, early_out, feat_width)))


def solution(mesh):
    return jax.shard_map(
        on_device,
        mesh=mesh,
        in_specs=(
            P(("grp", "bus"), None, None),
            P(("grp", "bus")),
            P(),
            P(),
            P("grp"),
            P(),
            P(),
            P(),
            P(),
            P("grp", None),
            P("grp", "bus", None),
        ),
        out_specs=(P("grp", "bus", None), P("grp", "bus", None)),
        check_vma=False,
    )
```

```python
import functools
import math

import jax
import jax.numpy as jnp
from jax import lax
from jax.experimental import pallas as pl
from jax.experimental.pallas import tpu as pltpu
from jax.sharding import PartitionSpec as P

EPSILON = 1e-05
NEG_FILL = -1e30
VMEM_LIMIT = 56 << 20
SETTLE_STEPS = 2
EARLY_PAIRS = 2
PLANE = 4


def nt_dot(a, b):
    return lax.dot_general(a, b, (((1,), (1,)), ((), ())), preferred_element_type=jnp.float32)


def tn_dot(a, b):
    return lax.dot_general(a, b, (((0,), (0,)), ((), ())), preferred_element_type=jnp.float32)


def encode_kernel(
    hour_ref, order_ref, series_ref, table_ref, gain_ref, wq_ref, wk_ref, wv_ref, q_ref, k_ref, v_ref
):
    tile = order_ref.shape[0]
    buses = series_ref.shape[0]
    hours = table_ref.shape[0]
    pick = lax.broadcasted_iota(jnp.int32, (tile, buses), 1) == order_ref[...]
    ordered = jnp.dot(
        pick.astype(jnp.bfloat16), series_ref[...], preferred_element_type=jnp.float32
    )
    table = table_ref[...].astype(jnp.float32)
    is_hour = lax.broadcasted_iota(jnp.int32, (hours, 1), 0) == hour_ref[0]
    hour_row = jnp.sum(jnp.where(is_hour, table, 0.0), axis=0, keepdims=True)
    mixed = ordered + hour_row
    power = jnp.mean(mixed * mixed, axis=1, keepdims=True)
    normed = (mixed * lax.rsqrt(power + EPSILON) * gain_ref[...]).astype(jnp.bfloat16)
    for weight_ref, out_ref in ((wq_ref, q_ref), (wk_ref, k_ref), (wv_ref, v_ref)):
        out_ref[...] = jnp.dot(
            normed, weight_ref[...], preferred_element_type=jnp.float32
        ).astype(jnp.bfloat16)


def encode(series, hour_ids, hour_table, norm_gain, order, w_query, w_key, w_value, tile):
    buses, width = series.shape
    feat = w_query.shape[1]
    whole = lambda shape: pl.BlockSpec(shape, lambda i, *_: (0, 0))
    row_spec = pl.BlockSpec((tile, feat), lambda i, *_: (i, 0))
    out = jax.ShapeDtypeStruct((buses, feat), jnp.bfloat16)
    return pl.pallas_call(
        encode_kernel,
        grid_spec=pltpu.PrefetchScalarGridSpec(
            num_scalar_prefetch=1,
            grid=(buses // tile,),
            in_specs=[
                pl.BlockSpec((tile, 1), lambda i, *_: (i, 0)),
                whole((buses, width)),
                whole(hour_table.shape),
                whole((1, width)),
                whole((width, feat)),
                whole((width, feat)),
                whole((width, feat)),
            ],
            out_specs=[row_spec, row_spec, row_spec],
        ),
        out_shape=[out, out, out],
        compiler_params=pltpu.CompilerParams(vmem_limit_bytes=VMEM_LIMIT),
        cost_estimate=pl.CostEstimate(
            flops=2 * buses * width * (buses + 3 * feat),
            bytes_accessed=2 * (buses * width + 3 * width * feat + 3 * buses * feat),
            transcendentals=buses,
        ),
        name="encode",
    )(
        hour_ids,
        order.reshape(buses, 1),
        series,
        hour_table,
        norm_gain.reshape(1, width),
        w_query,
        w_key,
        w_value,
    )


def both_heads(x):
    first_half = lax.broadcasted_iota(jnp.int32, x.shape, 1) < x.shape[1] // 2
    zero = jnp.zeros_like(x)
    return jnp.concatenate([jnp.where(first_half, x, zero), jnp.where(first_half, zero, x)], 0)


def tile_at(ref, block, rows):
    return ref[block * rows : (block + 1) * rows, :]


def near_tiles(ref, block, rows):
    last = ref.shape[0] // rows - 1
    near = (max(block - 1, 0), block, min(block + 1, last))
    return jnp.concatenate([tile_at(ref, c, rows) for c in near], 0)


def head_scales(scale_ref, rows):
    pair = pl.program_id(0)
    col = lax.broadcasted_iota(jnp.int32, (1, 2 * rows), 1)
    return jnp.where(col < rows, scale_ref[2 * pair], scale_ref[2 * pair + 1])


def softmax_over_keys(raw, scale, neighbors_ref, block, rows):
    scale_log2 = scale * math.log2(math.e)
    read = [neighbors_ref[block, d] >= 0 for d in range(3)]
    tiles = [raw[d * rows : (d + 1) * rows] for d in range(3)]
    tops = [
        jnp.where(ok, jnp.max(tile, axis=0, keepdims=True) * scale_log2, NEG_FILL)
        for ok, tile in zip(read, tiles)
    ]
    row_max = jnp.maximum(jnp.maximum(tops[0], tops[1]), tops[2])
    powers = jnp.concatenate(
        [
            jnp.exp2(tile * scale_log2 - jnp.where(ok, row_max, -NEG_FILL))
            for ok, tile in zip(read, tiles)
        ],
        0,
    )
    total = jnp.sum(powers, axis=0, keepdims=True)
    return powers * (1.0 / total), row_max + jnp.log2(total)


class KeySums:
    def __init__(self, out_ref, rows):
        self.out_ref, self.rows, self.open = out_ref, rows, [None, None]

    def store(self, block, value):
        self.out_ref[block * self.rows : (block + 1) * self.rows, :] = value.astype(jnp.bfloat16)

    def add(self, block, part):
        low, own, high = [part[d * self.rows : (d + 1) * self.rows] for d in range(3)]
        if block > 0:
            self.store(block - 1, self.open[0] + low)
            own = self.open[1] + own
        self.open = [own, high]

    def close(self, block):
        self.store(block, self.open[0])


def weights_kernel(
    rows, neighbors_ref, scale_ref, q_ref, k_ref, v_ref, w_ref, attended_ref, shift_ref
):
    blocks = q_ref.shape[0] // rows
    scale = head_scales(scale_ref, rows)

    def products(b):
        return nt_dot(near_tiles(k_ref, b, rows), both_heads(tile_at(q_ref, b, rows)))

    def attend(b, weights_b):
        attended = tn_dot(near_tiles(v_ref, b, rows), weights_b)
        attended_ref[0, b] = attended.astype(jnp.bfloat16)

    raw, last = products(0), None
    for b in range(blocks):
        ahead = products(b + 1) if b + 1 < blocks else None
        weights, shift = softmax_over_keys(raw, scale, neighbors_ref, b, rows)
        weights_b = weights.astype(jnp.bfloat16)
        w_ref[0, b] = weights_b
        shift_ref[0, b : b + 1] = shift
        if last is not None:
            attend(b - 1, last)
        raw, last = ahead, weights_b
    attend(blocks - 1, last)


def early_value_kernel(rows, me_ref, w_ref, g_ref, *rest):
    *outs, held = rest
    value_kernel(rows, w_ref, g_ref, held)
    for k, out in enumerate(outs):
        for i in range(PLANE):
            block = me_ref[0] ^ (PLANE * k + i)
            tile = held[pl.ds(pl.multiple_of(block * rows, rows), rows), :]
            out[i * rows : (i + 1) * rows, :] = tile


def value_kernel(rows, w_ref, g_ref, *rest):
    dv_ref = rest[-1]
    blocks = g_ref.shape[0] // rows
    sums = KeySums(dv_ref, rows)

    def products(b):
        g_two = both_heads(tile_at(g_ref, b, rows))
        return jnp.dot(w_ref[0, b], g_two, preferred_element_type=jnp.float32)

    part = products(0)
    for b in range(blocks):
        ahead = products(b + 1) if b + 1 < blocks else None
        sums.add(b, part)
        part = ahead
    sums.close(blocks - 1)


def key_kernel(
    rows, neighbors_ref, scale_ref, q_ref, k_ref, v_ref, g_ref, attended_ref, shift_ref, *rest
):
    dk_ref = rest[-1]
    blocks = q_ref.shape[0] // rows
    half = q_ref.shape[1] // 2
    scale = head_scales(scale_ref, rows)
    scale_log2 = scale * math.log2(math.e)
    sums = KeySums(dk_ref, rows)

    def products(b):
        q_two = both_heads(tile_at(q_ref, b, rows))
        g_two = both_heads(tile_at(g_ref, b, rows))
        raw = nt_dot(near_tiles(k_ref, b, rows), q_two)
        return q_two, raw, nt_dot(near_tiles(v_ref, b, rows), g_two)

    def finish(b, found):
        q_two, raw, dweights = found
        shift = shift_ref[0, b : b + 1]
        weights = jnp.concatenate(
            [
                jnp.exp2(
                    raw[d * rows : (d + 1) * rows] * scale_log2
                    - jnp.where(neighbors_ref[b, d] >= 0, shift, -NEG_FILL)
                )
                for d in range(3)
            ],
            0,
        )
        turned = tile_at(g_ref, b, rows).astype(jnp.float32).T
        attended = attended_ref[0, b].astype(jnp.float32)
        row_dot = jnp.concatenate(
            [
                jnp.sum(turned[:half] * attended[:half, :rows], axis=0, keepdims=True),
                jnp.sum(turned[half:] * attended[half:, rows:], axis=0, keepdims=True),
            ],
            1,
        )
        dscores = (weights * (dweights - row_dot) * scale).astype(jnp.bfloat16)
        return jnp.dot(dscores, q_two, preferred_element_type=jnp.float32)

    one, part = products(0), None
    for b in range(blocks):
        ahead = products(b + 1) if b + 1 < blocks else None
        now = finish(b, one)
        if part is not None:
            sums.add(b - 1, part)
        one, part = ahead, now
    sums.add(blocks - 1, part)
    sums.close(blocks - 1)


def settle_kernel(me_ref, x_ref, out_ref):
    out_ref[...] = x_ref[...]


def settle(me, swapped, feat):
    devices, rows, lanes = swapped.shape
    block = (1, rows, lanes)
    return pl.pallas_call(
        settle_kernel,
        grid_spec=pltpu.PrefetchScalarGridSpec(
            num_scalar_prefetch=1,
            grid=(devices,),
            in_specs=[pl.BlockSpec(block, lambda j, me_ref: (j, 0, 0))],
            out_specs=pl.BlockSpec(block, lambda j, me_ref: (me_ref[0] ^ j, 0, 0)),
        ),
        out_shape=pltpu.HBM((devices, rows, feat), jnp.bfloat16),
        compiler_params=pltpu.CompilerParams(vmem_limit_bytes=8 << 20),
        cost_estimate=pl.CostEstimate(flops=0, bytes_accessed=4 * swapped.size, transcendentals=0),
        name="settle",
    )(me, swapped)


def swap(value, bits):
    devices = lax.axis_size("bus")
    return lax.ppermute(value, "bus", [(i, i ^ bits) for i in range(devices)])


def swap_far(parts):
    return [parts[0]] + [swap(part, PLANE * k) for k, part in enumerate(parts) if k]


def swap_near(far):
    planes = len(far)
    up = swap(jnp.stack([entry[2:] for entry in far]), 2)
    right = swap(jnp.stack([jnp.stack([entry[1] for entry in far]), up[:, 1]], 1), 1)
    order = []
    for k in range(planes):
        order += [far[k][0], right[k, 0], up[k, 0], right[k, 1]]
    return jnp.stack(order)


def part_kernel(late_ref, _, dk_ref, dv_ref):
    lanes = dv_ref.shape[2]
    dv_ref[...] = late_ref[:, :, :lanes]
    dk_ref[...] = late_ref[:, :, lanes:]


def part(late, settled):
    devices, rows, feat = settled.shape
    width = late.shape[2]
    run = devices // math.gcd(devices, SETTLE_STEPS)
    out = pltpu.HBM(settled.shape, jnp.bfloat16)
    whole = pl.BlockSpec((run, rows, feat), lambda i: (i, 0, 0))
    last = (2 * feat - width) // (width - feat)
    return pl.pallas_call(
        part_kernel,
        grid=(devices // run,),
        in_specs=[
            pl.BlockSpec((run, rows, width), lambda i: (i, 0, 0)),
            pl.BlockSpec(memory_space=pl.ANY),
        ],
        out_specs=[whole, pl.BlockSpec((run, rows, width - feat), lambda i: (i, 0, last))],
        out_shape=[out, out],
        input_output_aliases={1: 1},
        compiler_params=pltpu.CompilerParams(vmem_limit_bytes=24 << 20),
        cost_estimate=pl.CostEstimate(flops=0, bytes_accessed=4 * late.size, transcendentals=0),
        name="part",
    )(late, settled)


def by_pair(
    kernel, name, rows, heads, feat, first, count, scalars, arrays, outs, out_first, dots, exps,
    into=None, limit=40, scratch=(),
):
    buses, lanes = arrays[1].shape[0], 2 * feat // heads

    def spec(shape, at):
        if len(shape) > 2:
            zeros = (0,) * (len(shape) - 1)
            return pl.BlockSpec((1,) + shape[1:], lambda p, *_: (at + p, *zeros))
        return pl.BlockSpec((shape[0], lanes), lambda p, *_: (0, at + p))

    specs = [spec(x.shape, first) for x in arrays]
    arrays, alias = list(arrays), {}
    if into is not None:
        alias = {len(scalars) + len(arrays): 0}
        specs.append(pl.BlockSpec(memory_space=pl.ANY))
        arrays.append(into)
    return pl.pallas_call(
        functools.partial(kernel, rows),
        grid_spec=pltpu.PrefetchScalarGridSpec(
            num_scalar_prefetch=len(scalars),
            grid=(count,),
            in_specs=specs,
            out_specs=[spec(x.shape, out_first) for x in outs],
            scratch_shapes=scratch,
        ),
        out_shape=[pltpu.HBM(x.shape, x.dtype) for x in outs],
        input_output_aliases=alias,
        compiler_params=pltpu.CompilerParams(vmem_limit_bytes=limit << 20),
        cost_estimate=pl.CostEstimate(
            flops=2 * dots * 3 * rows * buses * count * lanes,
            bytes_accessed=2 * count * heads // 2 * sum(math.prod(x.shape) for x in arrays),
            transcendentals=exps * 3 * rows * buses * 2 * count,
        ),
        name=name,
    )(*scalars, *arrays)


def on_device(
    series,
    hour_ids,
    hour_table,
    norm_gain,
    bus_order,
    w_query,
    w_key,
    w_value,
    score_scale,
    neighbors,
    grad_out,
):
    head_count = score_scale.shape[0]
    snap_count, block_rows, feat_width = grad_out.shape
    bus_count = series.shape[1]
    devices = lax.axis_size("bus")
    head_scale = score_scale / math.sqrt(feat_width // head_count)
    pairs, lanes = head_count // 2, 2 * feat_width // head_count
    early = EARLY_PAIRS
    me = lax.axis_index("bus").astype(jnp.int32).reshape(1)
    late = pairs - early

    def exchange(value):
        return lax.all_to_all(value, "bus", split_axis=0, concat_axis=0, tiled=True)

    def blocks_of(value):
        return value.reshape(devices, block_rows, value.shape[-1])

    scalars = (neighbors, head_scale)
    bus_blocks = bus_count // block_rows
    bf16 = lambda *shape: jax.ShapeDtypeStruct(shape, jnp.bfloat16)
    call = functools.partial(by_pair, rows=block_rows, heads=head_count, feat=feat_width)

    grads = exchange(grad_out).reshape(bus_count, feat_width)
    queries, keys, values = encode(
        series[0], hour_ids, hour_table, norm_gain, bus_order,
        w_query, w_key, w_value, math.gcd(bus_count, 256),
    )
    weights, attended, shifts = call(
        weights_kernel, "weights", limit=40, first=0, count=pairs, scalars=scalars,
        arrays=(queries, keys, values), out_first=0, dots=2, exps=1,
        outs=[
            bf16(pairs, bus_blocks, 3 * block_rows, 2 * block_rows),
            bf16(pairs, bus_blocks, lanes, 2 * block_rows),
            jax.ShapeDtypeStruct((pairs, bus_blocks, 2 * block_rows), jnp.float32),
        ],
    )
    early_value = call(
        early_value_kernel, "value_early", first=0, count=early, scalars=(me,),
        arrays=(weights, grads), out_first=0, dots=1, exps=0,
        outs=[bf16(PLANE * block_rows, early * lanes)] * (devices // PLANE),
        scratch=[pltpu.VMEM((bus_count, lanes), jnp.bfloat16)],
    )
    early_far = swap_far(
        [x.reshape(PLANE, block_rows, early * lanes) for x in early_value]
    )
    grads, _ = lax.optimization_barrier((grads, early_value))
    rest_out = bf16(bus_count, late * lanes + feat_width)
    (rest,) = call(
        value_kernel, "value_late", first=early, count=late, scalars=(),
        arrays=(weights, grads), outs=[rest_out], out_first=0, dots=1, exps=0,
    )
    (rest,) = call(
        key_kernel, "key", first=0, count=pairs, scalars=scalars,
        arrays=(queries, keys, values, grads, attended, shifts), outs=[rest_out],
        out_first=late, dots=3, exps=1, into=rest,
    )
    early_far, rest = lax.optimization_barrier((early_far, rest))
    late_out = exchange(blocks_of(rest))
    early_out = swap_near(early_far)
    return tuple(part(late_out, settle(me, early_out, feat_width)))


def solution(mesh):
    return jax.shard_map(
        on_device,
        mesh=mesh,
        in_specs=(
            P(("grp", "bus"), None, None),
            P(("grp", "bus")),
            P(),
            P(),
            P("grp"),
            P(),
            P(),
            P(),
            P(),
            P("grp", None),
            P("grp", "bus", None),
        ),
        out_specs=(P("grp", "bus", None), P("grp", "bus", None)),
        check_vma=False,
    )
```
